128 devices in a mesh: lat: 8 (over y, core), lon: 16 (over x, z).
Axes of the slice: x: 4, y: 4, z: 4, core: 2. Of those that a mesh axis runs over, the one named last changes fastest.
Arguments:
- field: bfloat16 [128, 256, 384], P('lat', 'lon'), may hold values from -6 to 6
- obs_jac: bfloat16 [128, 128, 128, 384], P(None, ('lat', 'lon')), may hold values from -0.3125 to 0.3125
- obs_frac: bfloat16 [128, 128, 2, 128], P(None, ('lat', 'lon')), may hold values from 0 to 1
- obs_innov: bfloat16 [128, 128, 128], P(None, ('lat', 'lon')), may hold values from -6 to 6
- obs_rinv: bfloat16 [128, 128, 128], P(None, ('lat', 'lon')), may hold values from 1 to 16
- obs_cells: int32 [128, 128, 128], P(None, ('lat', 'lon')), may hold values from -1 to 270, as said below
Outputs:
- departures: float32 [128, 128, 128], P(None, ('lat', 'lon'))
- field_grad: float32 [128, 256, 384], P('lat', 'lon')
The draws below stay inside these ranges and needn't reach their ends.
Inputs may be any that keep to these rules, and one draw needn't show every extreme that they name: `obs_cells`: in block (o, p) the live slots come first, at least one and at most 128; a live slot holds r * 17 + q with r below 16 and q below 16; slot 0 of every block holds the cell at r = 15, q = 15; the number of live slots varies by owner.
All inputs are finite; a program needn't handle non-finite values.
Results may differ from the reference program's by a relative error of at most 0.0046.
Values may be sent and summed in bfloat16 or wider, within the bound.
No kernel may reach another device: no remote copies, remote signals or barrier semaphores. Data moves between devices by JAX's collectives and lax.ppermute only.
A program may use at most 128 MiB of HBM per device.

```python
import math
import jax
import jax.numpy as jnp
from jax import lax

LAT_DEV = 16
LON_DEV = 16
SLOTS = 128
WIDTH = 384
NLAT = 128
NLON = 256
N_LON = 16
DEVICES = 128


def draw_obs_cells(key, part):
    key_level, key_cut, key_row, key_col, key_pick = jax.random.split(key, 5)
    level_vals = jax.random.randint(key_level, (DEVICES, 1), 1, 5)
    chosen = jax.random.permutation(key_pick, DEVICES)[0]
    level_vals = jnp.where(jnp.arange(DEVICES)[:, None] == chosen, 4, level_vals)
    cut_vals = jax.random.randint(key_cut, (DEVICES, DEVICES), 0, SLOTS // 4)
    live_count = SLOTS * level_vals // 4 - cut_vals
    first_src = jnp.arange(DEVICES)[None, :] == 0
    live_count = jnp.where(first_src & (level_vals == 4), SLOTS, live_count)
    row_vals = jax.random.randint(key_row, (DEVICES, DEVICES, SLOTS), 0, LAT_DEV)
    col_vals = jax.random.randint(key_col, (DEVICES, DEVICES, SLOTS), 0, LON_DEV)
    slot_idx = jnp.arange(SLOTS)[None, None, :]
    cell_vals = row_vals * (LON_DEV + 1) + col_vals
    cell_vals = jnp.where(slot_idx == 0, LAT_DEV * (LON_DEV + 1) - 2, cell_vals)
    cell_vals = jnp.where(slot_idx < live_count[:, :, None], cell_vals, -1)
    return cell_vals.astype(jnp.int32)


def block_levels(own_key, shape, cuts, smallest, largest):
    factor_of = 1.0
    for dim, parts in cuts:
        steps = jax.random.uniform(jax.random.fold_in(jax.random.fold_in(own_key, 6), dim), (parts,), jnp.float32, smallest / len(cuts), largest / len(cuts))
        factor_of = factor_of * jnp.repeat(jnp.exp(steps), shape[dim] // parts).reshape((-1,) + (1,) * (len(shape) - 1 - dim))
    return factor_of


def normal_values(key, shape, scale, reach, cuts=(), kind=jnp.bfloat16):
    values = jax.random.normal(key, shape, jnp.float32) * scale
    if len(cuts) > 0:
        values = block_levels(key, shape, cuts, -0.22, 0.18) * values
    return jnp.clip(values, min=-reach, max=reach).astype(kind)


def setup_inputs(seed: int = 0) -> dict:
    splits = jax.random.split(jax.random.key(seed), 7)
    return {
        "field": normal_values(splits[0], (NLAT, NLON, WIDTH), 1.0, 6.0, ((0, 8), (1, 16))),
        "obs_jac": normal_values(splits[1], (DEVICES, DEVICES, SLOTS, WIDTH), WIDTH ** -0.5, 0.3125, ((1, 128),)),
        "obs_frac": jnp.clip(1.0 * jax.random.uniform(splits[2], (DEVICES, DEVICES, 2, SLOTS), jnp.float32) ** block_levels(splits[2], (DEVICES, DEVICES, 2, SLOTS), ((1, 128),), -0.2, 0.2), 0.0, 1.0).astype(jnp.bfloat16),
        "obs_innov": normal_values(splits[3], (DEVICES, DEVICES, SLOTS), 1.0, 6.0, ((1, 128),)),
        "obs_rinv": jnp.clip(jnp.exp(math.log(16.0) - 2.7725887 * jax.random.uniform(splits[4], (DEVICES, DEVICES, SLOTS), jnp.float32) ** block_levels(splits[4], (DEVICES, DEVICES, SLOTS), ((1, 128),), -0.2, 0.2)), 1.0, 16.0).astype(jnp.bfloat16),
        "obs_cells": draw_obs_cells(jax.random.fold_in(splits[6], 71), 0),
    }


def local_terms(col_table, stride, cell_ids, frac_lat, frac_lon, innovation, inv_error, jacobian, grad_ext):
    is_live = cell_ids >= 0
    corner = jnp.where(is_live, cell_ids, 0).astype(jnp.int32)
    lat_part = frac_lat.astype(jnp.float32)
    lon_part = frac_lon.astype(jnp.float32)
    raw_weights = ((1.0 - lat_part) * (1.0 - lon_part), lat_part * (1.0 - lon_part), (1.0 - lat_part) * lon_part, lat_part * lon_part)
    rounded = lax.optimization_barrier(tuple(weight.astype(jnp.bfloat16) for weight in raw_weights))
    weights = tuple(weight.astype(jnp.float32) for weight in rounded)
    offsets = (0, stride, 1, stride + 1)
    interp = jnp.zeros((cell_ids.shape[0], col_table.shape[1]), jnp.float32)
    for weight, offset in zip(weights, offsets):
        interp = interp + weight[:, None] * col_table[corner + offset].astype(jnp.float32)
    jac_wide = jacobian.astype(jnp.float32)
    evolved = jnp.sum(interp * jac_wide, axis=1)
    departure = jnp.where(is_live, evolved - innovation.astype(jnp.float32), jnp.zeros((), jnp.float32))
    contrib_low = lax.optimization_barrier(((inv_error.astype(jnp.float32) * departure)[:, None] * jac_wide).astype(jnp.bfloat16))
    contrib = contrib_low.astype(jnp.float32)
    for weight, offset in zip(weights, offsets):
        grad_ext = grad_ext.at[corner + offset].add(weight[:, None] * contrib)
    return departure, grad_ext


def reference(field, obs_jac, obs_frac, obs_innov, obs_rinv, obs_cells):
    width_all = field.shape[2]
    stride = LON_DEV + 1
    extended = jnp.concatenate([field, field[:, :1]], axis=1)
    extended = jnp.concatenate([extended, jnp.zeros((1, NLON + 1, width_all), field.dtype)], axis=0)
    owners = jnp.arange(DEVICES, dtype=jnp.int32)

    def visit_owner(grad_all, pieces):
        owner_id, jac_rows, frac_pair, innov_vals, rinv_vals, cell_vals = pieces
        row_start = ((owner_id // N_LON) * LAT_DEV).astype(jnp.int32)
        col_start = ((owner_id % N_LON) * LON_DEV).astype(jnp.int32)
        zero_idx = jnp.zeros((), jnp.int32)
        col_table = lax.dynamic_slice(extended, (row_start, col_start, zero_idx), (LAT_DEV + 1, stride, width_all)).reshape(-1, width_all)
        local_grad = jnp.zeros(((LAT_DEV + 1) * stride, width_all), jnp.float32)
        departure, local_grad = local_terms(col_table, stride, cell_vals.reshape(-1), frac_pair[:, 0, :].reshape(-1), frac_pair[:, 1, :].reshape(-1), innov_vals.reshape(-1), rinv_vals.reshape(-1), jac_rows.reshape(-1, width_all), local_grad)
        old_grad = lax.dynamic_slice(grad_all, (row_start, col_start, zero_idx), (LAT_DEV + 1, stride, width_all))
        grad_all = lax.dynamic_update_slice(grad_all, old_grad + local_grad.reshape(LAT_DEV + 1, stride, width_all), (row_start, col_start, zero_idx))
        return grad_all, departure.reshape(cell_vals.shape)

    grad_all = jnp.zeros((NLAT + 1, NLON + 1, width_all), jnp.float32)
    grad_all, departures = lax.scan(visit_owner, grad_all, (owners, obs_jac, obs_frac, obs_innov, obs_rinv, obs_cells))
    field_grad = grad_all[:NLAT, :NLON].at[:, 0].add(grad_all[:NLAT, NLON])
    return departures, field_grad
```

```python
import functools

import jax
import jax.numpy as jnp
from jax import lax
from jax.experimental import pallas as pl
from jax.experimental.pallas import tpu as pltpu
from jax.sharding import PartitionSpec as P

FIRST_SLOTS = 104
TILE = 256
BLOCK = 1024


def shifted(block, axis, distance):
    devices = range(lax.axis_size(axis))
    route = [(i - distance, i) for i in devices if i - distance in devices]
    return lax.ppermute(block, axis, route)


def passed_along(value, axis, steps):
    count = lax.axis_size(axis)
    pairs = [(source, (source + steps) % count) for source in range(count)]
    return lax.ppermute(value, axis, pairs)


def passed_diagonally(value, steps):
    rows, cols = lax.axis_size("lat"), lax.axis_size("lon")
    pairs = [
        (i * cols + j, (i + steps) * cols + (j + steps) % cols)
        for i in range(rows)
        for j in range(cols)
        if 0 <= i + steps < rows
    ]
    return lax.ppermute(value, ("lat", "lon"), pairs)


def exchanged(block):
    return lax.all_to_all(block, ("lat", "lon"), split_axis=0, concat_axis=0, tiled=True)


def chunk_kernel(table, jac, meta, grad_in, depart, grad_out, spread, *, side):
    east = (side + 1) * side
    rows = table.shape[0] - east

    @pl.when(pl.program_id(0) == 0)
    def _():
        grad_out[...] = grad_in[...]

    place = lax.broadcasted_iota(jnp.int32, (rows, TILE), 0).astype(jnp.float32)
    for start in range(0, jac.shape[0], TILE):
        lanes = slice(start, start + TILE)
        frac_lat, frac_lon, innov, rinv, row, col = (meta[i : i + 1, lanes] for i in range(6))
        lat_part = jnp.where(
            place == row, 1.0 - frac_lat, jnp.where(place == row + 1.0, frac_lat, 0.0)
        )
        lon_part = jnp.where(
            place == col, 1.0 - frac_lon, jnp.where(place == col + 1.0, frac_lon, 0.0)
        )
        proj = lax.dot_general(
            table[...],
            jac[lanes, :],
            (((1,), (1,)), ((), ())),
            preferred_element_type=jnp.float32,
        )
        bands = [
            (lat_part[i : i + 1] * lon_part[:side]).astype(jnp.bfloat16) for i in range(side + 1)
        ]
        edge = (lon_part[side : side + 1] * lat_part).astype(jnp.bfloat16)
        total = jnp.zeros((side, TILE), jnp.float32)
        for i, band in enumerate(bands):
            total = total + band.astype(jnp.float32) * proj[i * side : (i + 1) * side]
        edge_total = edge.astype(jnp.float32) * proj[east:]
        evolved = jnp.sum(total, axis=0, keepdims=True) + jnp.sum(edge_total, axis=0, keepdims=True)
        departure = jnp.where(row >= 0.0, evolved - innov, 0.0)
        depart[0, :, lanes] = departure
        scale = rinv * departure
        for i, band in enumerate(bands):
            spread[i * side : (i + 1) * side, lanes] = (band.astype(jnp.float32) * scale).astype(
                jnp.bfloat16
            )
        spread[east:, lanes] = (edge.astype(jnp.float32) * scale).astype(jnp.bfloat16)
    grad_out[...] += jnp.dot(spread[...], jac[...], preferred_element_type=jnp.float32)


def run_chunk(table, jac, meta, grad_in, side):
    slots, width = jac.shape
    cells = table.shape[0]
    steps = slots // BLOCK
    depart, grad = pl.pallas_call(
        functools.partial(chunk_kernel, side=side),
        grid=(steps,),
        in_specs=[
            pl.BlockSpec((cells, width), lambda i: (0, 0)),
            pl.BlockSpec((BLOCK, width), lambda i: (i, 0)),
            pl.BlockSpec((8, BLOCK), lambda i: (0, i)),
            pl.BlockSpec((cells, width), lambda i: (0, 0)),
        ],
        out_specs=[
            pl.BlockSpec((1, 1, BLOCK), lambda i: (i, 0, 0)),
            pl.BlockSpec((cells, width), lambda i: (0, 0)),
        ],
        out_shape=[
            jax.ShapeDtypeStruct((steps, 1, BLOCK), jnp.float32),
            jax.ShapeDtypeStruct((cells, width), jnp.float32),
        ],
        scratch_shapes=[pltpu.VMEM((cells, BLOCK), jnp.bfloat16)],
        compiler_params=pltpu.CompilerParams(
            dimension_semantics=("arbitrary",), vmem_limit_bytes=40 << 20
        ),
    )(table, jac, meta, grad_in)
    return depart, grad


def shards(field, obs_jac, obs_frac, obs_innov, obs_rinv, obs_cells):
    side, _, width = field.shape
    stride = side + 1
    owners, _, slots, _ = obs_jac.shape
    cells = obs_cells.reshape(owners, slots)
    row = jnp.where(cells >= 0, cells // stride, -8)
    col = jnp.where(cells >= 0, cells % stride, -8)
    low = jnp.bfloat16
    meta = jnp.stack(
        [
            obs_frac[:, 0, 0],
            obs_frac[:, 0, 1],
            obs_innov[:, 0],
            obs_rinv[:, 0],
            row.astype(low),
            col.astype(low),
            jnp.zeros((owners, slots), low),
            jnp.zeros((owners, slots), low),
        ],
        axis=1,
    )
    meta = exchanged(meta)
    jac = obs_jac.reshape(owners, slots, width)
    first = exchanged(jac[:, :FIRST_SLOTS])
    second = exchanged(jac[:, FIRST_SLOTS:])

    north = shifted(field[0], "lat", -1)
    east = passed_along(field[:, 0], "lon", -1)
    corner = passed_diagonally(field[0, :1], -1)
    pad = jnp.zeros((side - 1, width), field.dtype)
    table = jnp.concatenate([field.reshape(side * side, width), north, east, corner, pad], axis=0)

    fields = meta.transpose(1, 0, 2).astype(jnp.float32)
    meta_first = fields[:, :, :FIRST_SLOTS].reshape(8, -1)
    meta_second = fields[:, :, FIRST_SLOTS:].reshape(8, -1)
    grad = jnp.zeros(table.shape, jnp.float32)
    depart_first, grad = run_chunk(table, first.reshape(-1, width), meta_first, grad, side)
    depart_second, grad = run_chunk(table, second.reshape(-1, width), meta_second, grad, side)

    departs = jnp.concatenate(
        [depart_first.reshape(owners, -1), depart_second.reshape(owners, -1)], axis=1
    )
    main = side * side
    grid = grad[:main].reshape(side, side, width)
    north_back = shifted(grad[main : main + side], "lat", 1)
    east_back = passed_along(grad[main + side : main + 2 * side], "lon", 1)
    corner_back = passed_diagonally(grad[main + 2 * side : main + 2 * side + 1], 1)
    departures = exchanged(departs[:, None, :])
    top = north_back + jnp.pad(corner_back, ((0, side - 1), (0, 0)))
    field_grad = grid.at[:, 0].add(east_back).at[0].add(top)
    return (departures, field_grad)


def solution(mesh):
    placed = (
        P("lat", "lon", None),
        P(None, ("lat", "lon"), None, None),
        P(None, ("lat", "lon"), None, None),
        P(None, ("lat", "lon"), None),
        P(None, ("lat", "lon"), None),
        P(None, ("lat", "lon"), None),
    )
    return jax.shard_map(
        shards,
        mesh=mesh,
        in_specs=placed,
        out_specs=(P(None, ("lat", "lon"), None), P("lat", "lon", None)),
        check_vma=False,
    )
```

```python
import functools

import jax
import jax.numpy as jnp
from jax import lax
from jax.experimental import pallas as pl
from jax.experimental.pallas import tpu as pltpu
from jax.sharding import PartitionSpec as P

SENDERS = 32


def shifted(block, axis, distance):
    devices = range(lax.axis_size(axis))
    route = [(i - distance, i) for i in devices if i - distance in devices]
    return lax.ppermute(block, axis, route)


def passed_along(value, axis, steps):
    count = lax.axis_size(axis)
    pairs = [(source, (source + steps) % count) for source in range(count)]
    return lax.ppermute(value, axis, pairs)


def passed_diagonally(value, steps):
    rows, cols = lax.axis_size("lat"), lax.axis_size("lon")
    pairs = [
        (i * cols + j, (i + steps) * cols + (j + steps) % cols)
        for i in range(rows)
        for j in range(cols)
        if 0 <= i + steps < rows
    ]
    return lax.ppermute(value, ("lat", "lon"), pairs)


def exchanged(block):
    return lax.all_to_all(block, ("lat", "lon"), split_axis=0, concat_axis=0, tiled=True)


def observe_kernel(table, jac, meta, depart, grad, spread, *, side):
    east = (side + 1) * side
    rows = table.shape[0] - east
    slots = meta.shape[2]
    tile = 2 * slots
    place = lax.broadcasted_iota(jnp.int32, (rows, tile), 0).astype(jnp.float32)
    for pair in range(meta.shape[0] // 2):
        lanes = slice(pair * tile, (pair + 1) * tile)
        fields = jnp.concatenate([meta[2 * pair], meta[2 * pair + 1]], axis=1).astype(jnp.float32)
        frac_lat, frac_lon, innov, rinv, row, col = (fields[i : i + 1] for i in range(6))
        lat_part = jnp.where(
            place == row, 1.0 - frac_lat, jnp.where(place == row + 1.0, frac_lat, 0.0)
        )
        lon_part = jnp.where(
            place == col, 1.0 - frac_lon, jnp.where(place == col + 1.0, frac_lon, 0.0)
        )
        proj = lax.dot_general(
            table[...],
            jac[lanes, :],
            (((1,), (1,)), ((), ())),
            preferred_element_type=jnp.float32,
        )
        bands = [
            (lat_part[i : i + 1] * lon_part[:side]).astype(jnp.bfloat16) for i in range(side + 1)
        ]
        edge = (lon_part[side : side + 1] * lat_part).astype(jnp.bfloat16)
        total = jnp.zeros((side, tile), jnp.float32)
        for i, band in enumerate(bands):
            total = total + band.astype(jnp.float32) * proj[i * side : (i + 1) * side]
        edge_total = edge.astype(jnp.float32) * proj[east:]
        evolved = jnp.sum(total, axis=0, keepdims=True) + jnp.sum(edge_total, axis=0, keepdims=True)
        departure = jnp.where(row >= 0.0, evolved - innov, 0.0)
        depart[2 * pair] = departure[:, :slots]
        depart[2 * pair + 1] = departure[:, slots:]
        scale = rinv * departure
        for i, band in enumerate(bands):
            spread[i * side : (i + 1) * side, lanes] = (band.astype(jnp.float32) * scale).astype(
                jnp.bfloat16
            )
        spread[east:, lanes] = (edge.astype(jnp.float32) * scale).astype(jnp.bfloat16)
    part = jnp.dot(spread[...], jac[...], preferred_element_type=jnp.float32)

    @pl.when(pl.program_id(0) == 0)
    def _():
        grad[...] = part

    @pl.when(pl.program_id(0) > 0)
    def _():
        grad[...] += part


def observe(table, jac, meta, side):
    cells, width = table.shape
    senders, fields, slots = meta.shape
    block = SENDERS * slots
    return pl.pallas_call(
        functools.partial(observe_kernel, side=side),
        grid=(senders // SENDERS,),
        in_specs=[
            pl.BlockSpec((cells, width), lambda i: (0, 0)),
            pl.BlockSpec((block, width), lambda i: (i, 0)),
            pl.BlockSpec((SENDERS, fields, slots), lambda i: (i, 0, 0)),
        ],
        out_specs=[
            pl.BlockSpec((SENDERS, 1, slots), lambda i: (i, 0, 0)),
            pl.BlockSpec((cells, width), lambda i: (0, 0)),
        ],
        out_shape=[
            jax.ShapeDtypeStruct((senders, 1, slots), jnp.float32),
            jax.ShapeDtypeStruct((cells, width), jnp.float32),
        ],
        scratch_shapes=[pltpu.VMEM((cells, block), jnp.bfloat16)],
        compiler_params=pltpu.CompilerParams(
            dimension_semantics=("arbitrary",), vmem_limit_bytes=32 << 20
        ),
    )(table, jac, meta)


def shards(field, obs_jac, obs_frac, obs_innov, obs_rinv, obs_cells):
    side, _, width = field.shape
    stride = side + 1
    owners, _, slots, _ = obs_jac.shape
    jac = exchanged(obs_jac.reshape(owners, slots, width)).reshape(owners * slots, width)
    cells = obs_cells.reshape(owners, slots)
    row = jnp.where(cells >= 0, cells // stride, -8)
    col = jnp.where(cells >= 0, cells % stride, -8)
    low = jnp.bfloat16
    meta = jnp.stack(
        [
            obs_frac[:, 0, 0],
            obs_frac[:, 0, 1],
            obs_innov[:, 0],
            obs_rinv[:, 0],
            row.astype(low),
            col.astype(low),
            jnp.zeros((owners, slots), low),
            jnp.zeros((owners, slots), low),
        ],
        axis=1,
    )
    north = shifted(field[0], "lat", -1)
    east = passed_along(field[:, 0], "lon", -1)
    corner = passed_diagonally(field[0, :1], -1)
    pad = jnp.zeros((side - 1, width), field.dtype)
    table = jnp.concatenate([field.reshape(side * side, width), north, east, corner, pad], axis=0)

    meta, table, jac = lax.optimization_barrier((meta, table, jac))
    meta = exchanged(meta)

    departs, grad = observe(table, jac, meta, side)
    departures = exchanged(departs)
    main = side * side
    grid = grad[:main].reshape(side, side, width)
    north_back = shifted(grad[main : main + side], "lat", 1)
    east_back = passed_along(grad[main + side : main + 2 * side], "lon", 1)
    corner_back = passed_diagonally(grad[main + 2 * side : main + 2 * side + 1], 1)
    top = north_back + jnp.pad(corner_back, ((0, side - 1), (0, 0)))
    field_grad = grid.at[:, 0].add(east_back).at[0].add(top)
    return (departures, field_grad)


def solution(mesh):
    placed = (
        P("lat", "lon", None),
        P(None, ("lat", "lon"), None, None),
        P(None, ("lat", "lon"), None, None),
        P(None, ("lat", "lon"), None),
        P(None, ("lat", "lon"), None),
        P(None, ("lat", "lon"), None),
    )
    return jax.shard_map(
        shards,
        mesh=mesh,
        in_specs=placed,
        out_specs=(P(None, ("lat", "lon"), None), P("lat", "lon", None)),
        check_vma=False,
    )
```

```python
import functools

import jax
import jax.numpy as jnp
from jax import lax
from jax.experimental import pallas as pl
from jax.experimental.pallas import tpu as pltpu
from jax.sharding import PartitionSpec as P

SENDERS = 32


def shifted(block, axis, distance):
    devices = range(lax.axis_size(axis))
    route = [(i - distance, i) for i in devices if i - distance in devices]
    return lax.ppermute(block, axis, route)


def passed_along(value, axis, steps):
    count = lax.axis_size(axis)
    pairs = [(source, (source + steps) % count) for source in range(count)]
    return lax.ppermute(value, axis, pairs)


def passed_diagonally(value, steps):
    rows, cols = lax.axis_size("lat"), lax.axis_size("lon")
    pairs = [
        (i * cols + j, (i + steps) * cols + (j + steps) % cols)
        for i in range(rows)
        for j in range(cols)
        if 0 <= i + steps < rows
    ]
    return lax.ppermute(value, ("lat", "lon"), pairs)


def exchanged(block):
    return lax.all_to_all(block, ("lat", "lon"), split_axis=0, concat_axis=0, tiled=True)


def metadata_kernel(frac, innov, rinv, cells, meta, *, stride):
    cell = cells[...].astype(jnp.float32)
    row = ((cell + 0.5) * (1.0 / stride)).astype(jnp.int32).astype(jnp.float32)
    col = cell - stride * row
    live = cell >= 0.0
    row = jnp.where(live, row, -8.0)
    col = jnp.where(live, col, -8.0)
    both = frac[...].astype(jnp.float32)
    none = jnp.zeros_like(cell)
    fields = [
        both[:, 0],
        both[:, 1],
        innov[...].astype(jnp.float32),
        rinv[...].astype(jnp.float32),
        row,
        col,
        none,
        none,
    ]
    meta[...] = jnp.stack(fields, axis=1).astype(meta.dtype)


def metadata(frac, innov, rinv, cells, stride):
    owners, slots = cells.shape
    return pl.pallas_call(
        functools.partial(metadata_kernel, stride=stride),
        out_shape=jax.ShapeDtypeStruct((owners, 8, slots), frac.dtype),
    )(frac, innov, rinv, cells)


def observe_kernel(table, jac, meta, depart, grad, spread, *, side):
    east = (side + 1) * side
    rows = table.shape[0] - east
    slots = meta.shape[2]
    tile = 2 * slots
    place = lax.broadcasted_iota(jnp.int32, (rows, tile), 0).astype(jnp.float32)
    for pair in range(meta.shape[0] // 2):
        lanes = slice(pair * tile, (pair + 1) * tile)
        fields = jnp.concatenate([meta[2 * pair], meta[2 * pair + 1]], axis=1).astype(jnp.float32)
        frac_lat, frac_lon, innov, rinv, row, col = (fields[i : i + 1] for i in range(6))
        lat_part = jnp.where(
            place == row, 1.0 - frac_lat, jnp.where(place == row + 1.0, frac_lat, 0.0)
        )
        lon_part = jnp.where(
            place == col, 1.0 - frac_lon, jnp.where(place == col + 1.0, frac_lon, 0.0)
        )
        proj = lax.dot_general(
            table[...],
            jac[lanes, :],
            (((1,), (1,)), ((), ())),
            preferred_element_type=jnp.float32,
        )
        bands = [
            (lat_part[i : i + 1] * lon_part[:side]).astype(jnp.bfloat16) for i in range(side + 1)
        ]
        edge = (lon_part[side : side + 1] * lat_part).astype(jnp.bfloat16)
        total = jnp.zeros((side, tile), jnp.float32)
        for i, band in enumerate(bands):
            total = total + band.astype(jnp.float32) * proj[i * side : (i + 1) * side]
        edge_total = edge.astype(jnp.float32) * proj[east:]
        evolved = jnp.sum(total, axis=0, keepdims=True) + jnp.sum(edge_total, axis=0, keepdims=True)
        departure = jnp.where(row >= 0.0, evolved - innov, 0.0)
        depart[2 * pair] = departure[:, :slots]
        depart[2 * pair + 1] = departure[:, slots:]
        scale = rinv * departure
        for i, band in enumerate(bands):
            spread[i * side : (i + 1) * side, lanes] = (band.astype(jnp.float32) * scale).astype(
                jnp.bfloat16
            )
        spread[east:, lanes] = (edge.astype(jnp.float32) * scale).astype(jnp.bfloat16)
    part = jnp.dot(spread[...], jac[...], preferred_element_type=jnp.float32)

    @pl.when(pl.program_id(0) == 0)
    def _():
        grad[...] = part

    @pl.when(pl.program_id(0) > 0)
    def _():
        grad[...] += part


def observe(table, jac, meta, side):
    cells, width = table.shape
    senders, fields, slots = meta.shape
    block = SENDERS * slots
    return pl.pallas_call(
        functools.partial(observe_kernel, side=side),
        grid=(senders // SENDERS,),
        in_specs=[
            pl.BlockSpec((cells, width), lambda i: (0, 0)),
            pl.BlockSpec((block, width), lambda i: (i, 0)),
            pl.BlockSpec((SENDERS, fields, slots), lambda i: (i, 0, 0)),
        ],
        out_specs=[
            pl.BlockSpec((SENDERS, 1, slots), lambda i: (i, 0, 0)),
            pl.BlockSpec((cells, width), lambda i: (0, 0)),
        ],
        out_shape=[
            jax.ShapeDtypeStruct((senders, 1, slots), jnp.float32),
            jax.ShapeDtypeStruct((cells, width), jnp.float32),
        ],
        scratch_shapes=[pltpu.VMEM((cells, block), jnp.bfloat16)],
        compiler_params=pltpu.CompilerParams(
            dimension_semantics=("arbitrary",), vmem_limit_bytes=32 << 20
        ),
    )(table, jac, meta)


def shards(field, obs_jac, obs_frac, obs_innov, obs_rinv, obs_cells):
    side, _, width = field.shape
    stride = side + 1
    owners, _, slots, _ = obs_jac.shape
    meta = exchanged(
        metadata(
            obs_frac.reshape(owners, 2, slots),
            obs_innov.reshape(owners, slots),
            obs_rinv.reshape(owners, slots),
            obs_cells.reshape(owners, slots),
            stride,
        )
    )
    north = shifted(field[0], "lat", -1)
    east = passed_along(jnp.concatenate([field[:, 0], north[:1]], axis=0), "lon", -1)
    pad = jnp.zeros((side - 1, width), field.dtype)
    table = jnp.concatenate([field.reshape(side * side, width), north, east, pad], axis=0)
    meta, table, obs_jac = lax.optimization_barrier((meta, table, obs_jac))
    jac = exchanged(obs_jac.reshape(owners, slots, width)).reshape(owners * slots, width)

    departs, grad = observe(table, jac, meta, side)
    departures = exchanged(departs)
    main = side * side
    grid = grad[:main].reshape(side, side, width)
    east_back = passed_along(grad[main + side : main + 2 * side + 1], "lon", 1)
    north_row = grad[main : main + side]
    north_row = north_row + jnp.pad(east_back[side:], ((0, side - 1), (0, 0)))
    north_back = shifted(north_row, "lat", 1)
    field_grad = grid.at[:, 0].add(east_back[:side]).at[0].add(north_back)
    return (departures, field_grad)


def solution(mesh):
    placed = (
        P("lat", "lon", None),
        P(None, ("lat", "lon"), None, None),
        P(None, ("lat", "lon"), None, None),
        P(None, ("lat", "lon"), None),
        P(None, ("lat", "lon"), None),
        P(None, ("lat", "lon"), None),
    )
    return jax.shard_map(
        shards,
        mesh=mesh,
        in_specs=placed,
        out_specs=(P(None, ("lat", "lon"), None), P("lat", "lon", None)),
        check_vma=False,
    )
```

```python
import functools

import jax
import jax.numpy as jnp
from jax import lax
from jax.experimental import pallas as pl
from jax.experimental.pallas import tpu as pltpu
from jax.sharding import PartitionSpec as P

SENDERS = 64
LANES = 128


def shifted(block, axis, distance):
    devices = range(lax.axis_size(axis))
    route = [(i - distance, i) for i in devices if i - distance in devices]
    return lax.ppermute(block, axis, route)


def passed_along(value, axis, steps):
    count = lax.axis_size(axis)
    pairs = [(source, (source + steps) % count) for source in range(count)]
    return lax.ppermute(value, axis, pairs)


def passed_diagonally(value, steps):
    rows, cols = lax.axis_size("lat"), lax.axis_size("lon")
    pairs = [
        (i * cols + j, (i + steps) * cols + (j + steps) % cols)
        for i in range(rows)
        for j in range(cols)
        if 0 <= i + steps < rows
    ]
    return lax.ppermute(value, ("lat", "lon"), pairs)


def exchanged(block):
    return lax.all_to_all(block, ("lat", "lon"), split_axis=0, concat_axis=0, tiled=True)


def pack_kernel(jac, frac, innov, rinv, cells, packed, sems, *, stride):
    owners, slots, width = jac.shape
    groups, strips = sems.shape
    group = owners // groups
    copies = [
        pltpu.make_async_copy(
            jac.at[pl.ds(i * group, group), :, pl.ds(j * LANES, LANES)],
            packed.at[pl.ds(i * group, group), pl.ds(j * slots, slots)],
            sems.at[i, j],
        )
        for i in range(groups)
        for j in range(strips)
    ]
    for copy in copies:
        copy.start()
    cell = cells[...].astype(jnp.float32)
    row = ((cell + 0.5) * (1.0 / stride)).astype(jnp.int32).astype(jnp.float32)
    col = cell - stride * row
    live = cell >= 0.0
    row = jnp.where(live, row, -8.0)
    col = jnp.where(live, col, -8.0)
    both = frac[...].astype(jnp.float32)
    none = jnp.zeros_like(cell)
    fields = [
        both[:, 0],
        both[:, 1],
        innov[...].astype(jnp.float32),
        rinv[...].astype(jnp.float32),
        row,
        col,
        none,
        none,
    ]
    packed[:, strips * slots :] = jnp.stack(fields, axis=1).astype(packed.dtype)
    for copy in copies:
        copy.wait()


def pack(jac, frac, innov, rinv, cells, stride):
    owners, slots, width = jac.shape
    strips = width // LANES
    return pl.pallas_call(
        functools.partial(pack_kernel, stride=stride),
        in_specs=[pl.BlockSpec(memory_space=pltpu.HBM)] + [pl.BlockSpec()] * 4,
        out_specs=pl.BlockSpec(memory_space=pltpu.VMEM),
        out_shape=jax.ShapeDtypeStruct((owners, strips * slots + 8, LANES), jac.dtype),
        scratch_shapes=[pltpu.SemaphoreType.DMA((4, strips))],
        compiler_params=pltpu.CompilerParams(vmem_limit_bytes=8 << 20),
    )(*(pltpu.with_memory_space_constraint(x, pltpu.HBM) for x in (jac, frac, innov, rinv, cells)))


def observe_kernel(table, packed, depart_all, grad, spread, *, side):
    east = (side + 1) * side
    rows = table.shape[0] - east
    strips = table.shape[1] // LANES
    slots = (packed.shape[1] - 8) // strips
    tile = 2 * slots
    block = SENDERS * slots
    place = lax.broadcasted_iota(jnp.int32, (rows, tile), 0).astype(jnp.float32)

    def turn(step):
        own = packed.at[pl.ds(step * SENDERS, SENDERS)]
        depart = depart_all.at[pl.ds(step * SENDERS, SENDERS)]
        for pair in range(SENDERS // 2):
            lanes = slice(pair * tile, (pair + 1) * tile)
            meta = own[2 * pair : 2 * pair + 2, strips * slots :].astype(jnp.float32)
            fields = jnp.concatenate([meta[0], meta[1]], axis=1)
            jac = jnp.concatenate(
                [
                    own[2 * pair : 2 * pair + 2, j * slots : (j + 1) * slots].reshape(tile, LANES)
                    for j in range(strips)
                ],
                axis=1,
            )
            frac_lat, frac_lon, innov, rinv, row, col = (fields[i : i + 1] for i in range(6))
            lat_part = jnp.where(
                place == row, 1.0 - frac_lat, jnp.where(place == row + 1.0, frac_lat, 0.0)
            )
            lon_part = jnp.where(
                place == col, 1.0 - frac_lon, jnp.where(place == col + 1.0, frac_lon, 0.0)
            )
            proj = lax.dot_general(
                table[...],
                jac,
                (((1,), (1,)), ((), ())),
                preferred_element_type=jnp.float32,
            )
            bands = [
                (lat_part[i : i + 1] * lon_part[:side]).astype(jnp.bfloat16) for i in range(side + 1)
            ]
            edge = (lon_part[side : side + 1] * lat_part).astype(jnp.bfloat16)
            total = jnp.zeros((side, tile), jnp.float32)
            for i, band in enumerate(bands):
                total = total + band.astype(jnp.float32) * proj[i * side : (i + 1) * side]
            edge_total = edge.astype(jnp.float32) * proj[east:]
            evolved = jnp.sum(total, axis=0, keepdims=True) + jnp.sum(edge_total, axis=0, keepdims=True)
            departure = jnp.where(row >= 0.0, evolved - innov, 0.0)
            depart[2 * pair] = departure[:, :slots]
            depart[2 * pair + 1] = departure[:, slots:]
            scale = rinv * departure
            for i, band in enumerate(bands):
                spread[i * side : (i + 1) * side, lanes] = (band.astype(jnp.float32) * scale).astype(
                    jnp.bfloat16
                )
            spread[east:, lanes] = (edge.astype(jnp.float32) * scale).astype(jnp.bfloat16)

        jac = jnp.concatenate(
            [
                own[:, j * slots : (j + 1) * slots].reshape(block, LANES)
                for j in range(strips)
            ],
            axis=1,
        )
        part = jnp.dot(spread[...], jac, preferred_element_type=jnp.float32)
        grad[...] += part

    grad[...] = jnp.zeros_like(grad)
    lax.fori_loop(0, packed.shape[0] // SENDERS, lambda step, _: (turn(step), 0)[1], 0)


def observe(table, packed, side):
    cells, width = table.shape
    senders, slots = packed.shape[0], (packed.shape[1] - 8) * LANES // width
    block = SENDERS * slots
    whole = pl.BlockSpec(memory_space=pltpu.VMEM)
    return pl.pallas_call(
        functools.partial(observe_kernel, side=side),
        in_specs=[whole, whole],
        out_specs=[whole, whole],
        out_shape=[
            jax.ShapeDtypeStruct((senders, 1, slots), jnp.float32),
            jax.ShapeDtypeStruct((cells, width), jnp.float32),
        ],
        scratch_shapes=[pltpu.VMEM((cells, block), jnp.bfloat16)],
        compiler_params=pltpu.CompilerParams(vmem_limit_bytes=24 << 20),
    )(table, packed)


def shards(field, obs_jac, obs_frac, obs_innov, obs_rinv, obs_cells):
    side, _, width = field.shape
    stride = side + 1
    owners, _, slots, _ = obs_jac.shape
    packed = pack(
        obs_jac.reshape(owners, slots, width),
        obs_frac.reshape(owners, 2, slots),
        obs_innov.reshape(owners, slots),
        obs_rinv.reshape(owners, slots),
        obs_cells.reshape(owners, slots),
        stride,
    )
    north = shifted(field[0], "lat", -1)
    east = passed_along(jnp.concatenate([field[:, 0], north[:1]], axis=0), "lon", -1)
    pad = jnp.zeros((side - 1, width), field.dtype)
    table = jnp.concatenate([field.reshape(side * side, width), north, east, pad], axis=0)
    packed, table = lax.optimization_barrier((packed, table))
    packed = exchanged(packed)

    departs, grad = observe(table, packed, side)
    departures = exchanged(departs)
    main = side * side
    grid = grad[:main].reshape(side, side, width)
    east_back = passed_along(grad[main + side : main + 2 * side + 1], "lon", 1)
    north_row = grad[main : main + side]
    north_row = north_row + jnp.pad(east_back[side:], ((0, side - 1), (0, 0)))
    north_back = shifted(north_row, "lat", 1)
    field_grad = grid.at[:, 0].add(east_back[:side]).at[0].add(north_back)
    return (departures, field_grad)


def solution(mesh):
    placed = (
        P("lat", "lon", None),
        P(None, ("lat", "lon"), None, None),
        P(None, ("lat", "lon"), None, None),
        P(None, ("lat", "lon"), None),
        P(None, ("lat", "lon"), None),
        P(None, ("lat", "lon"), None),
    )
    return jax.shard_map(
        shards,
        mesh=mesh,
        in_specs=placed,
        out_specs=(P(None, ("lat", "lon"), None), P("lat", "lon", None)),
        check_vma=False,
    )
```
